256 devices in a mesh: dp: 32 (over z, y_lo, core), grp: 8 (over y_hi, x).
Axes of the slice: x: 4, y: 4 (y_hi: 2, y_lo: 2; y = y_hi * 2 + y_lo), z: 8, core: 2. Of those that a mesh axis runs over, the one named last changes fastest.
Arguments:
- activations: bfloat16 [16384, 3072], P('dp', 'grp'), may hold values from -125 to 125
- cotangents: bfloat16 [16384, 3072], P('dp', 'grp'), may hold values from -125 to 125
Outputs:
- update: float32 [3072, 3072], P('dp', 'grp')
The draws below stay inside these ranges and needn't reach their ends.
All inputs are finite; a program needn't handle non-finite values.
Results may differ from the reference program's by a relative error of at most 0.009.
Values may be sent and summed in bfloat16 or wider, within the bound.
No kernel may reach another device: no remote copies, remote signals or barrier semaphores. Data moves between devices by JAX's collectives and lax.ppermute only.
A program may use at most 128 MiB of HBM per device.

```python
import math
import jax
import jax.numpy as jnp
from jax import lax

D = 3072
R = 512
ITERS = 3
ROWS = 16384
N_DP = 32


def draw_scaled(key, stream_salt):
    base_key = jax.random.fold_in(key, stream_salt)
    values_key, column_key, row_key = jax.random.split(base_key, 3)
    rising = jnp.exp(math.log(3.0) * jnp.arange(D, dtype=jnp.float32) / D)
    column_scale = jnp.exp(jax.random.uniform(column_key, (D,), jnp.float32) * math.log(10.0)) * rising
    row_scale = jnp.exp(jax.random.uniform(row_key, (ROWS, 1), jnp.float32) * math.log(10.0))
    fluctuation = jax.random.truncated_normal(values_key, -4.0, 4.0, (ROWS, D), jnp.float32)
    return fluctuation * row_scale * column_scale / 10.0


def draw_activations(key, part):
    return draw_scaled(key, 11).astype(jnp.bfloat16)


def draw_cotangents(key, part):
    return draw_scaled(key, 23).astype(jnp.bfloat16)


def setup_inputs(seed: int = 0) -> dict:
    arg_keys = jax.random.split(jax.random.key(seed), 3)
    activations = draw_activations(jax.random.fold_in(arg_keys[2], 71), 0)
    cotangents = draw_cotangents(jax.random.fold_in(arg_keys[2], 71), 0)
    return {"activations": activations, "cotangents": cotangents}


damping = 0.05
epsilon = 1e-06

def block_terms(activations, cotangents, block_index):
    start_row = block_index * R
    inputs = lax.dynamic_slice_in_dim(activations, start_row, R, 0)
    grads = lax.dynamic_slice_in_dim(cotangents, start_row, R, 0)
    results = []
    for left_side, right_side in ((inputs, inputs), (grads, grads), (grads, inputs)):
        product = jnp.dot(left_side.T, right_side, preferred_element_type=jnp.float32)
        results.append(product)
    return results

def inverse_factor(covariance):
    identity = jnp.eye(D, dtype=jnp.float32)
    trace_sum = jnp.trace(covariance)
    damp_term = damping * trace_sum / D
    norm_square = jnp.sum(covariance * covariance) + 2.0 * damp_term * trace_sum + D * damp_term * damp_term
    scale_factor = lax.rsqrt(norm_square)
    base_matrix = (scale_factor * (covariance + damp_term * identity)).astype(jnp.bfloat16)
    iterate = (2.0 * identity - base_matrix.astype(jnp.float32)).astype(jnp.bfloat16)
    for sweep_index in range(ITERS - 1):
        product = jnp.dot(base_matrix, iterate, preferred_element_type=jnp.float32).astype(jnp.bfloat16)
        iterate = (2.0 * iterate.astype(jnp.float32) - jnp.dot(iterate, product, preferred_element_type=jnp.float32)).astype(jnp.bfloat16)
    return iterate

def reference(activations, cotangents):

    def add_block(totals, block_index):
        results = block_terms(activations, cotangents, block_index)
        return ((totals[0] + results[0], totals[1] + results[1], totals[2] + results[2]), None)
    zero_matrix = jnp.zeros((D, D), jnp.float32)
    sums, unused = lax.scan(add_block, (zero_matrix, zero_matrix, zero_matrix), jnp.arange(N_DP, dtype=jnp.int32))
    cov_inputs, cov_grads, gradient = sums
    inverse_inputs = inverse_factor(cov_inputs)
    inverse_grads = inverse_factor(cov_grads)
    left_side = jnp.dot(inverse_grads, gradient.astype(jnp.bfloat16), preferred_element_type=jnp.float32).astype(jnp.bfloat16)
    preconditioned = jnp.dot(left_side, inverse_inputs, preferred_element_type=jnp.float32)
    return preconditioned * lax.rsqrt(jnp.mean(preconditioned * preconditioned) + epsilon)
```

```python
import itertools
import jax
import jax.numpy as jnp
from jax import lax
from jax.sharding import Mesh
from jax.sharding import PartitionSpec as P

D = 3072
AXES = ("z", "l", "k", "h", "x")
damping = 0.05
epsilon = 1e-06
bf16 = jnp.bfloat16
f32 = jnp.float32


def permute(t, axes, move):
    axes = tuple(a for a in AXES if a in axes)
    sizes = [lax.axis_size(a) for a in axes]

    def flat(c):
        r = 0
        for ci, s in zip(c, sizes):
            r = r * s + ci
        return r

    pairs = []
    for c in itertools.product(*[range(s) for s in sizes]):
        d = move(dict(zip(axes, c)))
        if d is not None:
            pairs.append((flat(c), flat([d[a] for a in axes])))
    return lax.ppermute(t, axes if len(axes) > 1 else axes[0], pairs)


def shift(t, axis, by):
    n = lax.axis_size(axis)
    if by % n == 0:
        return t
    return permute(t, (axis,), lambda c: {axis: (c[axis] + by) % n})


def tdot(a, b):
    return lax.dot_general(a, b, (((0,), (0,)), ((), ())), preferred_element_type=f32)


def dot(a, b):
    return jnp.dot(a, b, preferred_element_type=f32)


def absolute(pieces, index, n):
    out = jnp.zeros((n, *pieces[0].shape), pieces[0].dtype)
    for j, p in enumerate(pieces):
        out = lax.dynamic_update_index_in_dim(out, p, (index - j) % n, 0)
    return out


def gather_x(u):
    return [u, shift(u, "x", 1), shift(u, "x", 2), shift(u, "x", 3)]


def gather_z(u):
    up, down = [u], [u]
    for _ in range(3):
        up.append(shift(up[-1], "z", 1))
        down.append(shift(down[-1], "z", 7))
    half = u.shape[0] // 2
    mid = jnp.concatenate([shift(up[-1][:half], "z", 1), shift(down[-1][half:], "z", 7)], 0)
    return up + [mid] + down[:0:-1]


def shards(act, cot):
    z, l, k, h, x = (lax.axis_index(a) for a in AXES)
    same = k == h
    own = jnp.stack([act, cot])
    blocks = gather_x(own)
    other = shift(own, "h", 1)
    blocks2 = [shift(b, "k", 1) for b in blocks]
    other2 = shift(other, "k", 1)
    right = jnp.where(same, own, other)
    right2 = jnp.where(same, blocks2[0], other2)
    parts = []
    for b, b2 in zip(blocks, blocks2):
        fa = tdot(b[0], right[0]) + tdot(b2[0], right2[0])
        fg = tdot(b[1], right[1]) + tdot(b2[1], right2[1])
        fw = tdot(b[1], right[0]) + tdot(b2[1], right2[0])
        parts.append(jnp.stack([fa, fg, fw]).astype(bf16))
    part = jnp.stack(parts)
    part = jnp.moveaxis(part.reshape(4, 3, 8, 48, 384), 2, 0)
    tile = lax.psum_scatter(part, "z", scatter_dimension=0, tiled=False)
    fa, fg, fw = tile[:, 0], tile[:, 1], tile[:, 2]
    mine = jnp.where(l == 0, fa, fg)
    sent = shift(jnp.where(l == 0, fg, fa), "l", 1)
    mine = (mine.astype(f32) + sent.astype(f32)).astype(bf16)
    fw = fw.astype(f32) + shift(fw, "l", 1).astype(f32)

    ta, tb = mine[:2], mine[2:]
    u = absolute(gather_z(ta.reshape(96, 384)), z, 8).reshape(8, 2, 48, 384)
    u = jnp.moveaxis(u, 0, 1).reshape(2, 384, 384)
    v = shift(u, "h", 1)
    u = jnp.stack([jnp.where(same, u, v), jnp.where(same, v, u)])
    got_a = [gather_x(u)[-j % 4] for j in range(4)]
    g = gather_x(tb)
    g = [g[-c % 4] for c in range(4)]
    v = shift(jnp.stack(g), "h", 1)
    g = jnp.stack(g)
    g = jnp.stack([jnp.where(same, g, v), jnp.where(same, v, g)])
    got_b = jnp.moveaxis(absolute(gather_z(g.reshape(768, 384)), z, 8).reshape(8, 2, 4, 2, 48, 384), 0, 3).reshape(2, 4, 2, 384, 384)
    halves = []
    for hf in range(2):
        cols = []
        for c in range(4):
            rows = [None] * 4
            for j in range(2):
                rows[(c - j) % 4] = got_a[c][hf, j]
                rows[(c - j - 2) % 4] = got_b[hf, c, j]
            cols.append(jnp.concatenate(rows, 0))
        halves.append(jnp.concatenate(cols, 1))
    f_own, f_oth = halves

    w_own = f_own.astype(f32)
    w_oth = f_oth.astype(f32)
    eye = lax.broadcasted_iota(jnp.int32, (1536, 1536), 0) == lax.broadcasted_iota(jnp.int32, (1536, 1536), 1)
    trace = jnp.sum(jnp.where(eye, w_own, 0.0))
    square = jnp.sum(w_own * w_own + w_oth * w_oth)
    both = jnp.stack([jnp.full((8, 128), trace), jnp.full((8, 128), square)])
    both = both + shift(both, "k", 1)
    trace, square = both[0, :1, :1], both[1, :1, :1]
    damp = damping * trace / D
    scale = lax.rsqrt(square + 2.0 * damp * trace + D * damp * damp)

    grad = [shift(fw[j], "x", -j) for j in range(4)]
    grad = jnp.concatenate(grad, 1)
    rows = 384 * z + 192 * h + 48 * x + lax.broadcasted_iota(jnp.int32, (48, 1536), 0)
    cid = lax.broadcasted_iota(jnp.int32, (48, 1536), 1)
    cols = 1536 * k + (cid // 384 + x) % 4 * 384 + cid % 384
    start = jnp.where(l == 0, grad, (rows == cols).astype(f32))
    y = start
    for _ in range(7):
        yb = y.astype(bf16)
        yo = shift(yb, "k", 1)
        prod = dot(yb, f_own) + dot(yo, f_oth)
        y = start + y - scale * (prod + damp * y)
    yb = y.astype(bf16)

    zc = yb.reshape(48, 4, 384)
    zp = jnp.stack([shift(zc[:, j], "x", j) for j in range(4)])
    swapped = permute(zp, ("k", "h"), lambda c: {"k": 1 - c["k"], "h": 1 - c["h"]} if c["k"] != c["h"] else None)
    zp = jnp.where(same, zp, swapped)
    from0 = permute(zp, ("l",), lambda c: {"l": 1} if c["l"] == 0 else None)
    zp = jnp.where(l == 0, zp, from0)
    zall = absolute([zp] + [shift(zp, "z", j) for j in range(1, 8)], z, 8)
    zall = jnp.moveaxis(zall, 0, 1).reshape(4, 384, 384)
    def p1(c):
        return None if c["l"] == 0 else {"l": c["h"], "h": c["h"]}
    def p2(c):
        return None if c["l"] == 0 else {"l": c["h"], "h": 1 - c["h"]}
    w1 = permute(yb, ("l", "h"), p1)
    w2 = permute(yb, ("l", "h"), p2)
    wp = jnp.where(l == h, w1, w2)
    wx = gather_x(wp)
    al = []
    for j in range(4):
        blk = wx[j].reshape(48, 4, 384)
        al.append(jnp.stack([blk[:, (j - i) % 4] for i in range(4)], 0))
    wal = absolute(al, x, 4)
    wal = jnp.moveaxis(wal, 0, 1).reshape(4, 192, 384)
    acc = sum(dot(wal[i], zall[i]) for i in range(4))
    acc = acc.reshape(2, 96, 384)
    keep = lax.dynamic_index_in_dim(acc, k, 0, keepdims=False)
    give = lax.dynamic_index_in_dim(acc, 1 - k, 0, keepdims=False)
    pre = keep + shift(give, "k", 1)
    total = jnp.full((8, 128), jnp.sum(pre * pre))
    total = lax.psum(total, ("l", "k"))
    n = lax.axis_size(("z", "h", "x"))
    total = jnp.sum(lax.all_to_all(jnp.broadcast_to(total, (n, 8, 128)), ("z", "h", "x"), split_axis=0, concat_axis=0, tiled=True), 0)
    return pre * lax.rsqrt(total[:1, :1] / (D * D) + epsilon)


def solution(mesh):
    split = Mesh(mesh.devices.reshape(8, 2, 2, 2, 4), AXES)
    return jax.shard_map(
        shards,
        mesh=split,
        in_specs=(P(("z", "l", "k"), ("h", "x")),) * 2,
        out_specs=P(("z", "l", "k"), ("h", "x")),
        check_vma=False,
    )
```

```python
import itertools
import jax
import jax.numpy as jnp
from jax import lax
from jax.experimental import pallas as pl
from jax.experimental.pallas import tpu as pltpu
from jax.sharding import Mesh
from jax.sharding import PartitionSpec as P

D = 3072
NA = 16
STEPS = 7
UNROLL = 7
AXES = ("z", "l", "k", "h", "x")
damping = 0.05
epsilon = 1e-06
bf16 = jnp.bfloat16
f32 = jnp.float32


def permute(t, axes, move):
    axes = tuple(a for a in AXES if a in axes)
    sizes = [lax.axis_size(a) for a in axes]

    def flat(c):
        r = 0
        for ci, s in zip(c, sizes):
            r = r * s + ci
        return r

    pairs = []
    for c in itertools.product(*[range(s) for s in sizes]):
        d = move(dict(zip(axes, c)))
        if d is not None:
            pairs.append((flat(c), flat([d[a] for a in axes])))
    return lax.ppermute(t, axes if len(axes) > 1 else axes[0], pairs)


def shift(t, axis, by):
    n = lax.axis_size(axis)
    if by % n == 0:
        return t
    return permute(t, (axis,), lambda c: {axis: (c[axis] + by) % n})


def tdot(a, b):
    return lax.dot_general(a, b, (((0,), (0,)), ((), ())), preferred_element_type=f32)


def dot(a, b):
    return jnp.dot(a, b, preferred_element_type=f32)


def absolute(pieces, index, n):
    out = jnp.zeros((n, *pieces[0].shape), pieces[0].dtype)
    for j, p in enumerate(pieces):
        out = lax.dynamic_update_index_in_dim(out, p, (index - j) % n, 0)
    return out


def gather_x(u):
    return [u, shift(u, "x", 1), shift(u, "x", 2), shift(u, "x", 3)]


def assemble_kernel(*refs):
    a_refs, b_ref = refs[:4], refs[4]
    own_ref, oth_ref, stats_ref, whole, sem_in, sem_out = refs[5:]
    loads, stores = [], []
    for hf in range(2):
        for r in range(4):
            for c in range(4):
                j = (c - r) % 4
                at = 16 * hf + 4 * r + c
                slabs, cols = pl.ds(8 * (4 * hf + r), 8), pl.ds(384 * c, 384)
                dst = whole.at[slabs, pl.ds(0, NA), cols]
                loads.append(pltpu.make_async_copy(a_refs[c].at[hf, :, j], dst, sem_in.at[2 * at]))
                dst = whole.at[slabs, pl.ds(NA, 48 - NA), cols]
                loads.append(pltpu.make_async_copy(b_ref.at[:, c, hf, j], dst, sem_in.at[2 * at + 1]))
    for cp in loads:
        cp.start()
    row = lax.broadcasted_iota(jnp.int32, (16, 384), 0)
    col = lax.broadcasted_iota(jnp.int32, (16, 384), 1)
    stats_ref[...] = jnp.zeros_like(stats_ref)
    for hf in range(2):
        for r in range(4):
            base = 8 * (4 * hf + r)
            for i in range(8):
                loads[8 * (4 * hf + r) + i].wait()
            out = (own_ref, oth_ref)[hf].at[pl.ds(8 * r, 8)]
            store = pltpu.make_async_copy(whole.at[pl.ds(base, 8)], out, sem_out.at[4 * hf + r])
            store.start()
            stores.append(store)

            def add(i, acc):
                sq, tr = acc
                for t in range(3):
                    v = whole[base + i, 16 * t : 16 * t + 16, :].astype(f32)
                    sq = sq + v * v
                    if hf == 0:
                        d = whole[base + i, 16 * t : 16 * t + 16, 384 * r : 384 * r + 384].astype(f32)
                        tr = tr + jnp.where(col == row + (48 * i + 16 * t), d, 0.0)
                return sq, tr

            zero = (jnp.zeros((16, 1536), f32), jnp.zeros((16, 384), f32))
            sq, tr = lax.fori_loop(0, 8, add, zero)
            sq = sum(sq[:, 128 * i : 128 * i + 128] for i in range(12))
            tr = sum(tr[:, 128 * i : 128 * i + 128] for i in range(3))
            stats_ref[0:8, :] += tr[:8] + tr[8:]
            stats_ref[8:16, :] += sq[:8] + sq[8:]
    for cp in stores:
        cp.wait()


def assemble(got_a, got_b):
    anywhere = pl.BlockSpec(memory_space=pl.ANY)
    half = jax.ShapeDtypeStruct((32, 48, 1536), bf16)
    own, oth, stats = pl.pallas_call(
        assemble_kernel,
        out_shape=(half, half, jax.ShapeDtypeStruct((16, 128), f32)),
        in_specs=[anywhere] * 5,
        out_specs=(anywhere, anywhere, pl.BlockSpec(memory_space=pltpu.VMEM)),
        scratch_shapes=[
            pltpu.VMEM((64, 48, 1536), bf16),
            pltpu.SemaphoreType.DMA((64,)),
            pltpu.SemaphoreType.DMA((8,)),
        ],
        compiler_params=pltpu.CompilerParams(vmem_limit_bytes=16 * 2**20),
        cost_estimate=pl.CostEstimate(flops=10**7, bytes_accessed=19 * 10**6, transcendentals=0),
    )(*got_a, got_b)
    return own.reshape(1536, 1536), oth.reshape(1536, 1536), stats


def shards(act, cot):
    z, l, k, h, x = (lax.axis_index(a) for a in AXES)
    same = k == h
    own = jnp.concatenate([act, cot], 1)
    up, down = shift(own, "x", 1), shift(own, "x", 3)
    other = shift(own, "h", 1)
    far = jnp.concatenate([shift(up[:256], "x", 1), shift(down[256:], "x", 3)], 0)
    blocks = [own, up, far, down]
    blocks2 = [shift(b, "k", 1) for b in blocks]
    other2 = shift(other, "k", 1)
    right = jnp.where(same, own, other)
    right2 = jnp.where(same, blocks2[0], other2)
    parts = []
    for b, b2 in zip(blocks, blocks2):
        p = (tdot(b, right) + tdot(b2, right2)).astype(bf16)
        parts.append(jnp.stack([p[:384, :384], p[384:, 384:], p[384:, :384]]).reshape(3, 8, 48, 384))
    part = jnp.moveaxis(jnp.stack(parts), 2, 0)
    tile = lax.psum_scatter(part, "z", scatter_dimension=0, tiled=False)
    fa, fg, fw = tile[:, 0], tile[:, 1], tile[:, 2]
    mine = jnp.where(l == 0, fa, fg)
    sent = shift(jnp.where(l == 0, fg, fa), "l", 1)
    mine = (mine.astype(f32) + sent.astype(f32)).astype(bf16)

    ta, tb = mine[:, :NA], mine[:, NA:]
    v = shift(tb, "h", 1)
    g = jnp.stack([jnp.where(same, tb, v), jnp.where(same, v, tb)])
    g = gather_x(g)
    g = jnp.stack([g[-c % 4] for c in range(4)])
    fw, g = lax.optimization_barrier((fw, g))
    got_b = lax.all_gather(g, "z", axis=0, tiled=False)
    u = lax.all_gather(ta, "z", axis=0, tiled=False)
    v = shift(u, "h", 1)
    u = jnp.stack([jnp.where(same, u, v), jnp.where(same, v, u)])
    left, right = shift(u, "x", 1), shift(u, "x", 3)
    across = jnp.concatenate([shift(left[:1], "x", 1), shift(right[1:], "x", 3)], 0)
    got_a = [u, right, across, left]
    fw = fw.astype(f32) + shift(fw, "l", 1).astype(f32)
    f_own, f_oth, stats = assemble(got_a, got_b)
    trace, square = jnp.sum(stats[:8]), jnp.sum(stats[8:])
    both = jnp.stack([jnp.full((8, 128), trace), jnp.full((8, 128), square)])
    both = both + shift(both, "k", 1)
    trace, square = both[0, :1, :1], both[1, :1, :1]
    damp = damping * trace / D
    scale = lax.rsqrt(square + 2.0 * damp * trace + D * damp * damp)

    grad = [shift(fw[j], "x", -j) for j in range(4)]
    grad = jnp.concatenate(grad, 1)
    rows = 384 * z + 192 * h + 48 * x + lax.broadcasted_iota(jnp.int32, (48, 1536), 0)
    cid = lax.broadcasted_iota(jnp.int32, (48, 1536), 1)
    cols = 1536 * k + (cid // 384 + x) % 4 * 384 + cid % 384
    start = jnp.where(l == 0, grad, (rows == cols).astype(f32))

    def step(_, y):
        yb = y.astype(bf16)
        yo = shift(yb, "k", 1)
        prod = dot(yb, f_own) + dot(yo, f_oth)
        return start + y - scale * (prod + damp * y)

    y = lax.fori_loop(0, STEPS, step, start, unroll=UNROLL)
    yb = y.astype(bf16)

    zc = yb.reshape(48, 4, 384)
    zp = jnp.stack([shift(zc[:, j], "x", j) for j in range(4)])
    zp = [permute(zp, ("l", "k", "h"), lambda c, t=t: {"l": t, "k": c["h"], "h": c["k"]} if c["l"] == 0 else None) for t in (0, 1)]
    zp = jnp.where(l == 0, zp[0], zp[1])
    zall = lax.all_gather(zp, "z", axis=1, tiled=True)
    def p1(c):
        return None if c["l"] == 0 else {"l": c["h"], "h": c["h"]}
    def p2(c):
        return None if c["l"] == 0 else {"l": c["h"], "h": 1 - c["h"]}
    w1 = permute(yb, ("l", "h"), p1)
    w2 = permute(yb, ("l", "h"), p2)
    wp = jnp.where(l == h, w1, w2)
    wx = gather_x(wp)
    al = []
    for j in range(4):
        blk = wx[j].reshape(48, 4, 384)
        al.append(jnp.stack([blk[:, (j - i) % 4] for i in range(4)], 0))
    wal = absolute(al, x, 4)
    wal = jnp.moveaxis(wal, 0, 1).reshape(4, 192, 384)
    acc = sum(dot(wal[i], zall[i]) for i in range(4))
    acc = acc.reshape(2, 96, 384)
    keep = lax.dynamic_index_in_dim(acc, k, 0, keepdims=False)
    give = lax.dynamic_index_in_dim(acc, 1 - k, 0, keepdims=False)
    pre = keep + shift(give, "k", 1)
    total = jnp.full((8, 128), jnp.sum(pre * pre))
    for rest in (("z", "l"), ("k", "h", "x")):
        copies = jnp.broadcast_to(total, (lax.axis_size(rest), 8, 128))
        total = jnp.sum(lax.all_to_all(copies, rest, split_axis=0, concat_axis=0, tiled=True), 0)
    return pre * lax.rsqrt(total[:1, :1] / (D * D) + epsilon)


def solution(mesh):
    split = Mesh(mesh.devices.reshape(8, 2, 2, 2, 4), AXES)
    return jax.shard_map(
        shards,
        mesh=split,
        in_specs=(P(("z", "l", "k"), ("h", "x")),) * 2,
        out_specs=P(("z", "l", "k"), ("h", "x")),
        check_vma=False,
    )
```

```python
import functools
import itertools
import jax
import jax.numpy as jnp
from jax import lax
from jax.experimental import pallas as pl
from jax.experimental.pallas import tpu as pltpu
from jax.sharding import Mesh
from jax.sharding import PartitionSpec as P

D = 3072
NA = 16
VLIM = 50
AXES = ("z", "l", "k", "h", "x")
damping = 0.05
epsilon = 1e-06
bf16 = jnp.bfloat16
f32 = jnp.float32


def permute(t, axes, move):
    axes = tuple(a for a in AXES if a in axes)
    sizes = [lax.axis_size(a) for a in axes]

    def flat(c):
        r = 0
        for ci, s in zip(c, sizes):
            r = r * s + ci
        return r

    pairs = []
    for c in itertools.product(*[range(s) for s in sizes]):
        d = move(dict(zip(axes, c)))
        if d is not None:
            pairs.append((flat(c), flat([d[a] for a in axes])))
    return lax.ppermute(t, axes if len(axes) > 1 else axes[0], pairs)


def shift(t, axis, by):
    n = lax.axis_size(axis)
    if by % n == 0:
        return t
    return permute(t, (axis,), lambda c: {axis: (c[axis] + by) % n})


def tdot(a, b):
    return lax.dot_general(a, b, (((0,), (0,)), ((), ())), preferred_element_type=f32)


def dot(a, b):
    return jnp.dot(a, b, preferred_element_type=f32)


def absolute(pieces, index, n):
    out = jnp.zeros((n, *pieces[0].shape), pieces[0].dtype)
    for j, p in enumerate(pieces):
        out = lax.dynamic_update_index_in_dim(out, p, (index - j) & (n - 1), 0)
    return out


def copies_over(t, axes):
    copies = jnp.broadcast_to(t, (lax.axis_size(axes), *t.shape))
    return lax.all_to_all(copies, axes, split_axis=0, concat_axis=0, tiled=True)


def products_kernel(js, *refs):
    n = len(js)
    b_refs, r_refs = refs[: 2 * n], refs[2 * n : 2 * n + 2]
    out_ref, turned, right, whole, sem = refs[-5:]
    for i in range(2):
        right[512 * i : 512 * i + 512, :] = r_refs[i][...]
    copies = []
    for t, j in enumerate(js):
        for i in range(2):
            b_ref = b_refs[2 * t + i]

            @pl.loop(0, 768, step=128)
            def _(m):
                at = pl.ds(pl.multiple_of(m, 128), 128)
                turned[at, 512 * i : 512 * i + 512] = b_ref[:, at].T

        @pl.loop(0, 3)
        def _(q):
            row = pl.multiple_of(384 * jnp.minimum(q, 1), 128)
            col = pl.multiple_of(384 * (q & 1), 128)
            p = dot(turned[pl.ds(row, 384), :], right[:, pl.ds(col, 384)])
            whole[3 * t + q] = p.astype(bf16).reshape(8, 48, 384)

        for q in range(3):
            copies.append(pltpu.make_async_copy(whole.at[3 * t + q], out_ref.at[:, q, j], sem.at[3 * t + q]))
            copies[-1].start()
    for cp in copies:
        cp.wait()


def products(js, part, *operands):
    vmem = pl.BlockSpec(memory_space=pltpu.VMEM)
    hbm = pl.BlockSpec(memory_space=pltpu.HBM)
    more = () if part is None else (part,)
    n = len(js)
    return pl.pallas_call(
        functools.partial(products_kernel, js),
        out_shape=pltpu.HBM((8, 3, 4, 48, 384), bf16),
        in_specs=[vmem] * len(operands) + [hbm] * len(more),
        out_specs=hbm,
        scratch_shapes=[
            pltpu.VMEM((768, 1024), bf16),
            pltpu.VMEM((1024, 768), bf16),
            pltpu.VMEM((3 * n, 8, 48, 384), bf16),
            pltpu.SemaphoreType.DMA((3 * n,)),
        ],
        input_output_aliases={len(operands): 0} if more else {},
        compiler_params=pltpu.CompilerParams(vmem_limit_bytes=24 * 2**20),
        cost_estimate=pl.CostEstimate(flops=9 * 10**8 * n, bytes_accessed=4 * 10**6 * n, transcendentals=0),
    )(*operands, *more)


def assemble_kernel(*refs):
    x_ref, a_refs, b_ref = refs[0], refs[1:5], refs[5]
    own_ref, oth_ref, stats_ref, sem_in = refs[6:]
    whole = (own_ref, oth_ref)
    x = x_ref[0]
    loads = []
    for hf in range(2):
        for r in range(4):
            for c in range(4):
                j = (c - r) % 4
                at = 16 * hf + 4 * r + c
                slabs, cols = pl.ds(8 * r, 8), pl.ds(384 * c, 384)
                dst = whole[hf].at[slabs, pl.ds(0, NA), cols]
                loads.append(pltpu.make_async_copy(a_refs[c].at[hf, :, j], dst, sem_in.at[2 * at]))
                dst = whole[hf].at[slabs, pl.ds(NA, 48 - NA), cols]
                loads.append(pltpu.make_async_copy(b_ref.at[:, lax.rem(x + c, 4), hf, j], dst, sem_in.at[2 * at + 1]))
    for cp in loads:
        cp.start()
    row = lax.broadcasted_iota(jnp.int32, (16, 384), 0)
    col = lax.broadcasted_iota(jnp.int32, (16, 384), 1)
    stats_ref[...] = jnp.zeros_like(stats_ref)
    for hf in range(2):
        for r in range(4):
            base = 8 * r
            for i in range(8):
                loads[8 * (4 * hf + r) + i].wait()

            def add(i, acc):
                sq, tr = acc
                for t in range(3):
                    v = whole[hf][base + i, 16 * t : 16 * t + 16, :].astype(f32)
                    sq = sq + v * v
                    if hf == 0:
                        d = whole[hf][base + i, 16 * t : 16 * t + 16, 384 * r : 384 * r + 384].astype(f32)
                        tr = tr + jnp.where(col == row + (48 * i + 16 * t), d, 0.0)
                return sq, tr

            zero = (jnp.zeros((16, 1536), f32), jnp.zeros((16, 384), f32))
            sq, tr = lax.fori_loop(0, 8, add, zero)
            sq = sum(sq[:, 128 * i : 128 * i + 128] for i in range(12))
            tr = sum(tr[:, 128 * i : 128 * i + 128] for i in range(3))
            stats_ref[0:8, :] += tr[:8] + tr[8:]
            stats_ref[8:16, :] += sq[:8] + sq[8:]


def assemble(x, got_a, got_b):
    hbm = pl.BlockSpec(memory_space=pltpu.HBM)
    half = pltpu.VMEM((32, 48, 1536), bf16)
    own, oth, stats = pl.pallas_call(
        assemble_kernel,
        out_shape=(half, half, jax.ShapeDtypeStruct((16, 128), f32)),
        in_specs=[pl.BlockSpec(memory_space=pltpu.SMEM)] + [hbm] * 5,
        out_specs=[pl.BlockSpec(memory_space=pltpu.VMEM)] * 3,
        scratch_shapes=[
            pltpu.SemaphoreType.DMA((64,)),
        ],
        compiler_params=pltpu.CompilerParams(vmem_limit_bytes=VLIM * 2**20),
        cost_estimate=pl.CostEstimate(flops=10**7, bytes_accessed=19 * 10**6, transcendentals=0),
    )(x.reshape(1), *got_a, got_b)
    return own, oth, stats


def own_kernel(yb_ref, f_ref, out_ref):
    @pl.loop(0, 1536, step=512)
    def _(i):
        at = pl.ds(pl.multiple_of(i, 512), 512)
        out_ref[:, at] = dot(yb_ref[...], f_ref[:, :, at].reshape(1536, 512))


def rest_kernel(st_ref, st2_ref, yb_ref, f_ref, part_ref, y_ref, start_ref, out_ref, outb_ref):
    st = st_ref[...] + st2_ref[...]
    trace = jnp.sum(st[:8], keepdims=True)
    square = jnp.sum(st[8:], keepdims=True)
    damp = damping * trace / D
    scale = lax.rsqrt(square + 2.0 * damp * trace + D * damp * damp)

    @pl.loop(0, 1536, step=512)
    def _(i):
        at = pl.ds(pl.multiple_of(i, 512), 512)
        prod = dot(yb_ref[...], f_ref[:, :, at].reshape(1536, 512)) + part_ref[:, at]
        y = y_ref[:, at]
        y = start_ref[:, at] + y - scale * (prod + damp * y)
        out_ref[:, at] = y
        outb_ref[:, at] = y.astype(bf16)


def step(stats, y, yb, start, f_own, f_oth):
    vmem = pl.BlockSpec(memory_space=pltpu.VMEM)
    limit = pltpu.CompilerParams(vmem_limit_bytes=16 * 2**20)
    cost = pl.CostEstimate(flops=2 * 48 * 1536 * 1536, bytes_accessed=6 * 10**6, transcendentals=0)
    yo = shift(yb, "k", 1)
    part = pl.pallas_call(
        own_kernel,
        out_shape=jax.ShapeDtypeStruct((48, 1536), f32),
        in_specs=[vmem] * 2,
        out_specs=vmem,
        compiler_params=limit,
        cost_estimate=cost,
    )(yb, f_own)
    return pl.pallas_call(
        rest_kernel,
        out_shape=(jax.ShapeDtypeStruct((48, 1536), f32), jax.ShapeDtypeStruct((48, 1536), bf16)),
        in_specs=[vmem] * 7,
        out_specs=(vmem, vmem),
        compiler_params=limit,
        cost_estimate=cost,
    )(*stats, yo, f_oth, part, y, start)


def shards(act, cot):
    z, l, k, h, x = (lax.axis_index(a) for a in AXES)
    same = k == h
    own = jnp.concatenate([act, cot], 1)
    up, down = shift(own, "x", 1), shift(own, "x", 3)
    other = shift(own, "h", 1)
    far = shift(up[:256], "x", 1), shift(down[256:], "x", 3)
    own2, up2, other2 = (shift(b, "k", 1) for b in (own, up, other))
    right = jnp.where(same, own, other)
    right2 = jnp.where(same, own2, other2)
    part = products((0, 1, 3), None, own, own2, up, up2, down, shift(down, "k", 1), right, right2)
    far, part = lax.optimization_barrier((far, part))
    far = jnp.concatenate(far, 0)
    part = products((2,), part, far, shift(far, "k", 1), right, right2)
    tile = lax.psum_scatter(part, "z", scatter_dimension=0, tiled=False)
    fa, fg, fw = tile[0], tile[1], tile[2]
    mine, give = jnp.where(l == 0, fa, fg), jnp.where(l == 0, fg, fa)
    diagonal = lambda c: {"l": 1 - c["l"], "h": 1 - c["h"]}
    sent = shift(give, "l", 1)
    near = shift(mine[:, NA:], "h", 1)
    sent_near = permute(give[:, NA:], ("l", "h"), diagonal)
    mine = (mine.astype(f32) + sent.astype(f32)).astype(bf16)
    v = (near.astype(f32) + sent_near.astype(f32)).astype(bf16)

    ta, tb = mine[:, :NA], mine[:, NA:]
    g = jnp.stack([jnp.where(same, tb, v), jnp.where(same, v, tb)])
    g = copies_over(g, "x")
    fw, g = lax.optimization_barrier((fw, g))
    got_b = lax.all_gather(g, "z", axis=0, tiled=False)
    u = lax.all_gather(ta, "z", axis=0, tiled=False)
    v = shift(u, "h", 1)
    u = jnp.stack([jnp.where(same, u, v), jnp.where(same, v, u)])
    left, right = shift(u, "x", 1), shift(u, "x", 3)
    across = jnp.concatenate([shift(left[:1], "x", 1), shift(right[1:], "x", 3)], 0)
    got_a = [u, right, across, left]
    fw = fw.astype(f32) + shift(fw, "l", 1).astype(f32)
    f_own, f_oth, stats = assemble(x, got_a, got_b)
    stats = (stats, shift(stats, "k", 1))

    grad = absolute([fw[j] for j in range(4)], x, 4)
    grad = lax.all_to_all(grad, "x", split_axis=0, concat_axis=0, tiled=True)
    grad = jnp.concatenate([grad[c % 4] for c in range(8)], 1)
    grad = lax.dynamic_slice_in_dim(grad, x * 384, 1536, 1)
    rows = 384 * z + 192 * h + 48 * x + lax.broadcasted_iota(jnp.int32, (48, 1536), 0)
    cid = lax.broadcasted_iota(jnp.int32, (48, 1536), 1)
    cols = 1536 * k + (cid // 384 + x) % 4 * 384 + cid % 384
    start = jnp.where(l == 0, grad, (rows == cols).astype(f32))

    y, yb = start, start.astype(bf16)
    for _ in range(7):
        y, yb = step(stats, y, yb, start, f_own, f_oth)

    x, k, l, same, yb = lax.optimization_barrier((x, k, l, same, yb))
    yb = lax.dynamic_slice_in_dim(jnp.concatenate([yb, yb], 1), (4 - x) * 384, 1536, 1)
    zp = jnp.stack([yb[:, 384 * c : 384 * c + 384] for c in range(4)])
    zp = lax.all_to_all(zp, "x", split_axis=0, concat_axis=0, tiled=True)
    zp = [permute(zp, ("l", "k", "h"), lambda c, t=t: {"l": t, "k": c["h"], "h": c["k"]} if c["l"] == 0 else None) for t in (0, 1)]
    zp = jnp.where(l == 0, zp[0], zp[1])
    zall = lax.all_gather(zp, "z", axis=1, tiled=True)
    def p1(c):
        return None if c["l"] == 0 else {"l": c["h"], "h": c["h"]}
    def p2(c):
        return None if c["l"] == 0 else {"l": c["h"], "h": 1 - c["h"]}
    w1 = permute(yb, ("l", "h"), p1)
    w2 = permute(yb, ("l", "h"), p2)
    wp = jnp.where(l == h, w1, w2)
    wx = copies_over(wp, "x")
    acc = dot(wx.reshape(192, 1536), zall.reshape(1536, 384))
    acc = acc.reshape(2, 96, 384)
    keep = lax.dynamic_index_in_dim(acc, k, 0, keepdims=False)
    give = lax.dynamic_index_in_dim(acc, 1 - k, 0, keepdims=False)
    pre = keep + shift(give, "k", 1)
    total = jnp.full((8, 128), jnp.sum(pre * pre))
    for rest in (("z", "l"), ("k", "h", "x")):
        total = jnp.sum(copies_over(total, rest), 0)
    return pre * lax.rsqrt(total[:1, :1] / (D * D) + epsilon)


def solution(mesh):
    split = Mesh(mesh.devices.reshape(8, 2, 2, 2, 4), AXES)
    return jax.shard_map(
        shards,
        mesh=split,
        in_specs=(P(("z", "l", "k"), ("h", "x")),) * 2,
        out_specs=P(("z", "l", "k"), ("h", "x")),
        check_vma=False,
    )
```

```python
import functools
import itertools
import jax
import jax.numpy as jnp
from jax import lax
from jax.experimental import pallas as pl
from jax.experimental.pallas import tpu as pltpu
from jax.sharding import Mesh
from jax.sharding import PartitionSpec as P

D = 3072
NA = 16
VLIM = 50
AXES = ("z", "l", "k", "h", "x")
damping = 0.05
epsilon = 1e-06
bf16 = jnp.bfloat16
f32 = jnp.float32


def permute(t, axes, move):
    axes = tuple(a for a in AXES if a in axes)
    sizes = [lax.axis_size(a) for a in axes]

    def flat(c):
        r = 0
        for ci, s in zip(c, sizes):
            r = r * s + ci
        return r

    pairs = []
    for c in itertools.product(*[range(s) for s in sizes]):
        d = move(dict(zip(axes, c)))
        if d is not None:
            pairs.append((flat(c), flat([d[a] for a in axes])))
    return lax.ppermute(t, axes if len(axes) > 1 else axes[0], pairs)


def shift(t, axis, by):
    n = lax.axis_size(axis)
    if by % n == 0:
        return t
    return permute(t, (axis,), lambda c: {axis: (c[axis] + by) % n})


def tdot(a, b):
    return lax.dot_general(a, b, (((0,), (0,)), ((), ())), preferred_element_type=f32)


def dot(a, b):
    return jnp.dot(a, b, preferred_element_type=f32)


def absolute(pieces, index, n):
    out = jnp.zeros((n, *pieces[0].shape), pieces[0].dtype)
    for j, p in enumerate(pieces):
        out = lax.dynamic_update_index_in_dim(out, p, (index - j) & (n - 1), 0)
    return out


def copies_over(t, axes):
    copies = jnp.broadcast_to(t, (lax.axis_size(axes), *t.shape))
    return lax.all_to_all(copies, axes, split_axis=0, concat_axis=0, tiled=True)


def products_kernel(js, *refs):
    n = len(js)
    b_refs, (r_ref, r2_ref) = refs[: 2 * n], refs[2 * n : 2 * n + 2]
    out_ref, whole, sem = refs[-3:]
    copies = []
    for t, j in enumerate(js):
        b_ref, b2_ref = b_refs[2 * t : 2 * t + 2]

        @pl.loop(0, 3)
        def _(q):
            at = pl.ds(pl.multiple_of(384 * jnp.minimum(q, 1), 128), 384)
            p = dot(b_ref[at, :], r_ref[q & 1]) + dot(b2_ref[at, :], r2_ref[q & 1])
            whole[3 * t + q] = p.astype(bf16).reshape(8, 48, 384)

        for q in range(3):
            copies.append(pltpu.make_async_copy(whole.at[3 * t + q], out_ref.at[:, q, j], sem.at[3 * t + q]))
            copies[-1].start()
    for cp in copies:
        cp.wait()


def products(js, part, *operands):
    vmem = pl.BlockSpec(memory_space=pltpu.VMEM)
    hbm = pl.BlockSpec(memory_space=pltpu.HBM)
    more = () if part is None else (part,)
    n = len(js)
    return pl.pallas_call(
        functools.partial(products_kernel, js),
        out_shape=pltpu.HBM((8, 3, 4, 48, 384), bf16),
        in_specs=[vmem] * len(operands) + [hbm] * len(more),
        out_specs=hbm,
        scratch_shapes=[
            pltpu.VMEM((3 * n, 8, 48, 384), bf16),
            pltpu.SemaphoreType.DMA((3 * n,)),
        ],
        input_output_aliases={len(operands): 0} if more else {},
        compiler_params=pltpu.CompilerParams(vmem_limit_bytes=24 * 2**20),
        cost_estimate=pl.CostEstimate(flops=9 * 10**8 * n, bytes_accessed=4 * 10**6 * n, transcendentals=0),
    )(*operands, *more)


def assemble_kernel(*refs):
    x_ref, a_refs, b_ref = refs[0], refs[1:5], refs[5]
    own_ref, oth_ref, stats_ref, sem_in = refs[6:]
    whole = (own_ref, oth_ref)
    x = x_ref[0]
    loads = []
    for hf in range(2):
        for r in range(4):
            for c in range(4):
                j = (c - r) % 4
                at = 16 * hf + 4 * r + c
                slabs, cols = pl.ds(8 * r, 8), pl.ds(384 * c, 384)
                dst = whole[hf].at[slabs, pl.ds(0, NA), cols]
                loads.append(pltpu.make_async_copy(a_refs[c].at[hf, :, j], dst, sem_in.at[2 * at]))
                dst = whole[hf].at[slabs, pl.ds(NA, 48 - NA), cols]
                loads.append(pltpu.make_async_copy(b_ref.at[:, lax.rem(x + c, 4), hf, j], dst, sem_in.at[2 * at + 1]))
    for cp in loads:
        cp.start()
    row = lax.broadcasted_iota(jnp.int32, (16, 384), 0)
    col = lax.broadcasted_iota(jnp.int32, (16, 384), 1)
    stats_ref[...] = jnp.zeros_like(stats_ref)
    for hf in range(2):
        for r in range(4):
            base = 8 * r
            for i in range(8):
                loads[8 * (4 * hf + r) + i].wait()

            def add(i, acc):
                sq, tr = acc
                for t in range(3):
                    v = whole[hf][base + i, 16 * t : 16 * t + 16, :].astype(f32)
                    sq = sq + v * v
                    if hf == 0:
                        d = whole[hf][base + i, 16 * t : 16 * t + 16, 384 * r : 384 * r + 384].astype(f32)
                        tr = tr + jnp.where(col == row + (48 * i + 16 * t), d, 0.0)
                return sq, tr

            zero = (jnp.zeros((16, 1536), f32), jnp.zeros((16, 384), f32))
            sq, tr = lax.fori_loop(0, 8, add, zero)
            sq = sum(sq[:, 128 * i : 128 * i + 128] for i in range(12))
            tr = sum(tr[:, 128 * i : 128 * i + 128] for i in range(3))
            stats_ref[0:8, :] += tr[:8] + tr[8:]
            stats_ref[8:16, :] += sq[:8] + sq[8:]


def assemble(x, got_a, got_b):
    hbm = pl.BlockSpec(memory_space=pltpu.HBM)
    half = pltpu.VMEM((32, 48, 1536), bf16)
    own, oth, stats = pl.pallas_call(
        assemble_kernel,
        out_shape=(half, half, jax.ShapeDtypeStruct((16, 128), f32)),
        in_specs=[pl.BlockSpec(memory_space=pltpu.SMEM)] + [hbm] * 5,
        out_specs=[pl.BlockSpec(memory_space=pltpu.VMEM)] * 3,
        scratch_shapes=[
            pltpu.SemaphoreType.DMA((64,)),
        ],
        compiler_params=pltpu.CompilerParams(vmem_limit_bytes=VLIM * 2**20),
        cost_estimate=pl.CostEstimate(flops=10**7, bytes_accessed=19 * 10**6, transcendentals=0),
    )(x.reshape(1), *got_a, got_b)
    return own, oth, stats


def own_kernel(yb_ref, f_ref, out_ref):
    @pl.loop(0, 1536, step=512)
    def _(i):
        at = pl.ds(pl.multiple_of(i, 512), 512)
        out_ref[:, at] = dot(yb_ref[...], f_ref[:, :, at].reshape(1536, 512))


def rest_kernel(st_ref, st2_ref, yb_ref, f_ref, part_ref, y_ref, start_ref, out_ref, outb_ref):
    st = st_ref[...] + st2_ref[...]
    trace = jnp.sum(st[:8], keepdims=True)
    square = jnp.sum(st[8:], keepdims=True)
    damp = damping * trace / D
    scale = lax.rsqrt(square + 2.0 * damp * trace + D * damp * damp)

    @pl.loop(0, 1536, step=512)
    def _(i):
        at = pl.ds(pl.multiple_of(i, 512), 512)
        prod = dot(yb_ref[...], f_ref[:, :, at].reshape(1536, 512)) + part_ref[:, at]
        y = y_ref[:, at]
        y = start_ref[:, at] + y - scale * (prod + damp * y)
        out_ref[:, at] = y
        outb_ref[:, at] = y.astype(bf16)


def step(stats, y, yb, start, f_own, f_oth):
    vmem = pl.BlockSpec(memory_space=pltpu.VMEM)
    limit = pltpu.CompilerParams(vmem_limit_bytes=16 * 2**20)
    cost = pl.CostEstimate(flops=2 * 48 * 1536 * 1536, bytes_accessed=6 * 10**6, transcendentals=0)
    yo = shift(yb, "k", 1)
    part = pl.pallas_call(
        own_kernel,
        out_shape=jax.ShapeDtypeStruct((48, 1536), f32),
        in_specs=[vmem] * 2,
        out_specs=vmem,
        compiler_params=limit,
        cost_estimate=cost,
    )(yb, f_own)
    return pl.pallas_call(
        rest_kernel,
        out_shape=(jax.ShapeDtypeStruct((48, 1536), f32), jax.ShapeDtypeStruct((48, 1536), bf16)),
        in_specs=[vmem] * 7,
        out_specs=(vmem, vmem),
        compiler_params=limit,
        cost_estimate=cost,
    )(*stats, yo, f_oth, part, y, start)


def shards(act, cot):
    z, l, k, h, x = (lax.axis_index(a) for a in AXES)
    same = k == h
    flat = jnp.stack([act, cot])
    own = jnp.concatenate([act.T, cot.T], 0)
    up, down = shift(own, "x", 1), shift(own, "x", 3)
    other = shift(flat, "h", 1)
    far = shift(up[:384], "x", 1), shift(down[384:], "x", 3)
    own2, up2, flat2, other2 = (shift(b, "k", 1) for b in (own, up, flat, other))
    right = jnp.where(same, flat, other)
    right2 = jnp.where(same, flat2, other2)
    part = products((0, 1, 3), None, own, own2, up, up2, down, shift(down, "k", 1), right, right2)
    far, part = lax.optimization_barrier((far, part))
    far = jnp.concatenate(far, 0)
    part = products((2,), part, far, shift(far, "k", 1), right, right2)
    tile = lax.psum_scatter(part, "z", scatter_dimension=0, tiled=False)
    fa, fg, fw = tile[0], tile[1], tile[2]
    mine, give = jnp.where(l == 0, fa, fg), jnp.where(l == 0, fg, fa)
    diagonal = lambda c: {"l": 1 - c["l"], "h": 1 - c["h"]}
    sent = shift(give, "l", 1)
    near = shift(mine[:, NA:], "h", 1)
    sent_near = permute(give[:, NA:], ("l", "h"), diagonal)
    sent, near, sent_near = lax.optimization_barrier((sent, near, sent_near))
    mine = (mine.astype(f32) + sent.astype(f32)).astype(bf16)
    v = (near.astype(f32) + sent_near.astype(f32)).astype(bf16)

    ta, tb = mine[:, :NA], mine[:, NA:]
    g = jnp.stack([jnp.where(same, tb, v), jnp.where(same, v, tb)])
    g = copies_over(g, "x")
    fw, g = lax.optimization_barrier((fw, g))
    got_b = lax.all_gather(g, "z", axis=0, tiled=False)
    u = lax.all_gather(ta, "z", axis=0, tiled=False)
    v = shift(u, "h", 1)
    u = jnp.stack([jnp.where(same, u, v), jnp.where(same, v, u)])
    left, right = shift(u, "x", 1), shift(u, "x", 3)
    across = jnp.concatenate([shift(left[:1], "x", 1), shift(right[1:], "x", 3)], 0)
    got_a = [u, right, across, left]
    fw = fw.astype(f32) + shift(fw, "l", 1).astype(f32)
    f_own, f_oth, stats = assemble(x, got_a, got_b)
    stats = (stats, shift(stats, "k", 1))

    grad = absolute([fw[j] for j in range(4)], x, 4)
    grad = lax.all_to_all(grad, "x", split_axis=0, concat_axis=0, tiled=True)
    grad = jnp.concatenate([grad[c % 4] for c in range(8)], 1)
    grad = lax.dynamic_slice_in_dim(grad, x * 384, 1536, 1)
    rows = 384 * z + 192 * h + 48 * x + lax.broadcasted_iota(jnp.int32, (48, 1536), 0)
    cid = lax.broadcasted_iota(jnp.int32, (48, 1536), 1)
    cols = 1536 * k + (cid // 384 + x) % 4 * 384 + cid % 384
    start = jnp.where(l == 0, grad, (rows == cols).astype(f32))

    y, yb = start, start.astype(bf16)
    for _ in range(7):
        y, yb = step(stats, y, yb, start, f_own, f_oth)

    x, k, l, same, yb = lax.optimization_barrier((x, k, l, same, yb))
    yb = lax.dynamic_slice_in_dim(jnp.concatenate([yb, yb], 1), (4 - x) * 384, 1536, 1)
    zp = jnp.stack([yb[:, 384 * c : 384 * c + 384] for c in range(4)])
    zp = lax.all_to_all(zp, "x", split_axis=0, concat_axis=0, tiled=True)
    zp = [permute(zp, ("l", "k", "h"), lambda c, t=t: {"l": t, "k": c["h"], "h": c["k"]} if c["l"] == 0 else None) for t in (0, 1)]
    zp = jnp.where(l == 0, zp[0], zp[1])
    zall = lax.all_gather(zp, "z", axis=1, tiled=True)
    def p1(c):
        return None if c["l"] == 0 else {"l": c["h"], "h": c["h"]}
    def p2(c):
        return None if c["l"] == 0 else {"l": c["h"], "h": 1 - c["h"]}
    w1 = permute(yb, ("l", "h"), p1)
    w2 = permute(yb, ("l", "h"), p2)
    wp = jnp.where(l == h, w1, w2)
    wx = copies_over(wp, "x")
    acc = dot(wx.reshape(192, 1536), zall.reshape(1536, 384))
    acc = acc.reshape(2, 96, 384)
    keep = lax.dynamic_index_in_dim(acc, k, 0, keepdims=False)
    give = lax.dynamic_index_in_dim(acc, 1 - k, 0, keepdims=False)
    pre = keep + shift(give, "k", 1)
    total = jnp.full((8, 128), jnp.sum(pre * pre))
    for rest in (("z", "l"), ("k", "h", "x")):
        total = jnp.sum(copies_over(total, rest), 0)
    return pre * lax.rsqrt(total[:1, :1] / (D * D) + epsilon)


def solution(mesh):
    split = Mesh(mesh.devices.reshape(8, 2, 2, 2, 4), AXES)
    return jax.shard_map(
        shards,
        mesh=split,
        in_specs=(P(("z", "l", "k"), ("h", "x")),) * 2,
        out_specs=P(("z", "l", "k"), ("h", "x")),
        check_vma=False,
    )
```

```python
import functools
import itertools
import jax
import jax.numpy as jnp
from jax import lax
from jax.experimental import pallas as pl
from jax.experimental.pallas import tpu as pltpu
from jax.sharding import Mesh
from jax.sharding import PartitionSpec as P

D = 3072
NA = 16
VLIM = 50
AXES = ("z", "l", "k", "h", "x")
damping = 0.05
epsilon = 1e-06
bf16 = jnp.bfloat16
f32 = jnp.float32


def permute(t, axes, move):
    axes = tuple(a for a in AXES if a in axes)
    sizes = [lax.axis_size(a) for a in axes]

    def flat(c):
        r = 0
        for ci, s in zip(c, sizes):
            r = r * s + ci
        return r

    pairs = []
    for c in itertools.product(*[range(s) for s in sizes]):
        d = move(dict(zip(axes, c)))
        if d is not None:
            pairs.append((flat(c), flat([d[a] for a in axes])))
    return lax.ppermute(t, axes if len(axes) > 1 else axes[0], pairs)


def shift(t, axis, by):
    n = lax.axis_size(axis)
    if by % n == 0:
        return t
    return permute(t, (axis,), lambda c: {axis: (c[axis] + by) % n})


def tdot(a, b):
    return lax.dot_general(a, b, (((0,), (0,)), ((), ())), preferred_element_type=f32)


def dot(a, b):
    return jnp.dot(a, b, preferred_element_type=f32)


def absolute(pieces, index, n):
    out = jnp.zeros((n, *pieces[0].shape), pieces[0].dtype)
    for j, p in enumerate(pieces):
        out = lax.dynamic_update_index_in_dim(out, p, (index - j) & (n - 1), 0)
    return out


def copies_over(t, axes):
    copies = jnp.broadcast_to(t, (lax.axis_size(axes), *t.shape))
    return lax.all_to_all(copies, axes, split_axis=0, concat_axis=0, tiled=True)


def products_kernel(js, *refs):
    n = len(js)
    b_refs, (r_ref, r2_ref) = refs[: 2 * n], refs[2 * n : 2 * n + 2]
    out_ref, whole, sem = refs[-3:]
    copies = []
    for t, j in enumerate(js):
        b_ref, b2_ref = b_refs[2 * t : 2 * t + 2]

        @pl.loop(0, 3)
        def _(q):
            at = pl.ds(pl.multiple_of(384 * jnp.minimum(q, 1), 128), 384)
            p = dot(b_ref[at, :], r_ref[q & 1]) + dot(b2_ref[at, :], r2_ref[q & 1])
            whole[3 * t + q] = p.astype(bf16).reshape(8, 48, 384)

        for q in range(3):
            copies.append(pltpu.make_async_copy(whole.at[3 * t + q], out_ref.at[:, q, j], sem.at[3 * t + q]))
            copies[-1].start()
    for cp in copies:
        cp.wait()


def products(js, part, *operands):
    vmem = pl.BlockSpec(memory_space=pltpu.VMEM)
    hbm = pl.BlockSpec(memory_space=pltpu.HBM)
    more = () if part is None else (part,)
    n = len(js)
    return pl.pallas_call(
        functools.partial(products_kernel, js),
        out_shape=pltpu.HBM((8, 3, 4, 48, 384), bf16),
        in_specs=[vmem] * len(operands) + [hbm] * len(more),
        out_specs=hbm,
        scratch_shapes=[
            pltpu.VMEM((3 * n, 8, 48, 384), bf16),
            pltpu.SemaphoreType.DMA((3 * n,)),
        ],
        input_output_aliases={len(operands): 0} if more else {},
        compiler_params=pltpu.CompilerParams(vmem_limit_bytes=24 * 2**20),
        cost_estimate=pl.CostEstimate(flops=9 * 10**8 * n, bytes_accessed=4 * 10**6 * n, transcendentals=0),
    )(*operands, *more)


def assemble_kernel(*refs):
    x_ref, a_refs, b_ref = refs[0], refs[1:5], refs[5]
    own_ref, oth_ref, stats_ref, sem_in = refs[6:]
    whole = (own_ref, oth_ref)
    x = x_ref[0]
    loads = []
    for hf in range(2):
        for r in range(4):
            for c in range(4):
                j = (c - r) % 4
                at = 16 * hf + 4 * r + c
                slabs, cols = pl.ds(8 * r, 8), pl.ds(384 * c, 384)
                dst = whole[hf].at[slabs, pl.ds(0, NA), cols]
                loads.append(pltpu.make_async_copy(a_refs[c].at[hf, :, j], dst, sem_in.at[2 * at]))
                dst = whole[hf].at[slabs, pl.ds(NA, 48 - NA), cols]
                loads.append(pltpu.make_async_copy(b_ref.at[:, lax.rem(x + c, 4), hf, j], dst, sem_in.at[2 * at + 1]))
    for cp in loads:
        cp.start()
    row = lax.broadcasted_iota(jnp.int32, (16, 384), 0)
    col = lax.broadcasted_iota(jnp.int32, (16, 384), 1)
    stats_ref[...] = jnp.zeros_like(stats_ref)
    for hf in range(2):
        for r in range(4):
            base = 8 * r
            for i in range(8):
                loads[8 * (4 * hf + r) + i].wait()

            def add(i, acc):
                sq, tr = acc
                for t in range(3):
                    v = whole[hf][base + i, 16 * t : 16 * t + 16, :].astype(f32)
                    sq = sq + v * v
                    if hf == 0:
                        d = whole[hf][base + i, 16 * t : 16 * t + 16, 384 * r : 384 * r + 384].astype(f32)
                        tr = tr + jnp.where(col == row + (48 * i + 16 * t), d, 0.0)
                return sq, tr

            zero = (jnp.zeros((16, 1536), f32), jnp.zeros((16, 384), f32))
            sq, tr = lax.fori_loop(0, 8, add, zero)
            sq = sum(sq[:, 128 * i : 128 * i + 128] for i in range(12))
            tr = sum(tr[:, 128 * i : 128 * i + 128] for i in range(3))
            stats_ref[0:8, :] += tr[:8] + tr[8:]
            stats_ref[8:16, :] += sq[:8] + sq[8:]


def assemble(x, got_a, got_b):
    hbm = pl.BlockSpec(memory_space=pltpu.HBM)
    half = pltpu.VMEM((32, 48, 1536), bf16)
    own, oth, stats = pl.pallas_call(
        assemble_kernel,
        out_shape=(half, half, jax.ShapeDtypeStruct((16, 128), f32)),
        in_specs=[pl.BlockSpec(memory_space=pltpu.SMEM)] + [hbm] * 5,
        out_specs=[pl.BlockSpec(memory_space=pltpu.VMEM)] * 3,
        scratch_shapes=[
            pltpu.SemaphoreType.DMA((64,)),
        ],
        compiler_params=pltpu.CompilerParams(vmem_limit_bytes=VLIM * 2**20),
        cost_estimate=pl.CostEstimate(flops=10**7, bytes_accessed=19 * 10**6, transcendentals=0),
    )(x.reshape(1), *got_a, got_b)
    return own, oth, stats


def own_kernel(yb_ref, f_ref, out_ref):
    @pl.loop(0, 1536, step=768)
    def _(i):
        at = pl.ds(pl.multiple_of(i, 768), 768)
        out_ref[:, at] = dot(yb_ref[...], f_ref[:, :, at].reshape(1536, 768))


def rest_kernel(first, *refs):
    if first:
        st_ref, st2_ref, yb_ref, f_ref, part_ref, y_ref, start_ref, out_ref, outb_ref, coef_ref = refs
        st = st_ref[...] + st2_ref[...]
        trace = jnp.sum(st[:8], keepdims=True)
        square = jnp.sum(st[8:], keepdims=True)
        damp = damping * trace / D
        scale = lax.rsqrt(square + 2.0 * damp * trace + D * damp * damp)
        coef_ref[0:8, :] = jnp.broadcast_to(scale, (8, 128))
        coef_ref[8:16, :] = jnp.broadcast_to(damp, (8, 128))
    else:
        coef_ref, yb_ref, f_ref, part_ref, y_ref, start_ref, out_ref, outb_ref = refs
        scale, damp = coef_ref[0:1, 0:1], coef_ref[8:9, 0:1]

    @pl.loop(0, 1536, step=512)
    def _(i):
        at = pl.ds(pl.multiple_of(i, 512), 512)
        prod = dot(yb_ref[...], f_ref[:, :, at].reshape(1536, 512)) + part_ref[:, at]
        y = y_ref[:, at]
        y = start_ref[:, at] + y - scale * (prod + damp * y)
        out_ref[:, at] = y
        outb_ref[:, at] = y.astype(bf16)


def step(coef, y, yb, start, f_own, f_oth):
    first = len(coef) == 2
    vmem = pl.BlockSpec(memory_space=pltpu.VMEM)
    limit = pltpu.CompilerParams(vmem_limit_bytes=16 * 2**20)
    cost = pl.CostEstimate(flops=2 * 48 * 1536 * 1536, bytes_accessed=6 * 10**6, transcendentals=0)
    yo = shift(yb, "k", 1)
    part = pl.pallas_call(
        own_kernel,
        out_shape=jax.ShapeDtypeStruct((48, 1536), f32),
        in_specs=[vmem] * 2,
        out_specs=vmem,
        compiler_params=limit,
        cost_estimate=cost,
    )(yb, f_own)
    outs = [jax.ShapeDtypeStruct((48, 1536), f32), jax.ShapeDtypeStruct((48, 1536), bf16)]
    if first:
        outs.append(jax.ShapeDtypeStruct((16, 128), f32))
    y, yb, *made = pl.pallas_call(
        functools.partial(rest_kernel, first),
        out_shape=outs,
        in_specs=[vmem] * (5 + len(coef)),
        out_specs=[vmem] * len(outs),
        compiler_params=limit,
        cost_estimate=cost,
    )(*coef, yo, f_oth, part, y, start)
    return (made if first else coef), y, yb


def shards(act, cot):
    z, l, k, h, x = (lax.axis_index(a) for a in AXES)
    same = k == h
    flat = jnp.stack([act, cot])
    own = jnp.concatenate([act.T, cot.T], 0)
    up, down = shift(own, "x", 1), shift(own, "x", 3)
    other = shift(flat, "h", 1)
    far = shift(up[:384], "x", 1), shift(down[384:], "x", 3)
    own2, up2, flat2, other2 = (shift(b, "k", 1) for b in (own, up, flat, other))
    right = jnp.where(same, flat, other)
    right2 = jnp.where(same, flat2, other2)
    part = products((0, 1, 3), None, own, own2, up, up2, down, shift(down, "k", 1), right, right2)
    far, part = lax.optimization_barrier((far, part))
    far = jnp.concatenate(far, 0)
    part = products((2,), part, far, shift(far, "k", 1), right, right2)
    tile = lax.psum_scatter(part, "z", scatter_dimension=0, tiled=False)
    fa, fg, fw = tile[0], tile[1], tile[2]
    mine, give = jnp.where(l == 0, fa, fg), jnp.where(l == 0, fg, fa)
    diagonal = lambda c: {"l": 1 - c["l"], "h": 1 - c["h"]}
    sent = shift(give, "l", 1)
    near = shift(mine[:, NA:], "h", 1)
    sent_near = permute(give[:, NA:], ("l", "h"), diagonal)
    sent, near, sent_near = lax.optimization_barrier((sent, near, sent_near))
    mine = (mine.astype(f32) + sent.astype(f32)).astype(bf16)
    v = (near.astype(f32) + sent_near.astype(f32)).astype(bf16)

    ta, tb = mine[:, :NA], mine[:, NA:]
    g = jnp.stack([jnp.where(same, tb, v), jnp.where(same, v, tb)])
    g = copies_over(g, "x")
    fw, g = lax.optimization_barrier((fw, g))
    got_b = lax.all_gather(g, "z", axis=0, tiled=False)
    u = lax.all_gather(ta, "z", axis=0, tiled=False)
    v = shift(u, "h", 1)
    u = jnp.stack([jnp.where(same, u, v), jnp.where(same, v, u)])
    left, right = shift(u, "x", 1), shift(u, "x", 3)
    across = jnp.concatenate([shift(left[:1], "x", 1), shift(right[1:], "x", 3)], 0)
    got_a = [u, right, across, left]
    fw = fw.astype(f32) + shift(fw, "l", 1).astype(f32)
    f_own, f_oth, stats = assemble(x, got_a, got_b)
    stats = (stats, shift(stats, "k", 1))

    grad = absolute([fw[j] for j in range(4)], x, 4)
    grad = lax.all_to_all(grad, "x", split_axis=0, concat_axis=0, tiled=True)
    grad = jnp.concatenate([grad[c % 4] for c in range(8)], 1)
    grad = lax.dynamic_slice_in_dim(grad, x * 384, 1536, 1)
    rows = 384 * z + 192 * h + 48 * x + lax.broadcasted_iota(jnp.int32, (48, 1536), 0)
    cid = lax.broadcasted_iota(jnp.int32, (48, 1536), 1)
    cols = 1536 * k + (cid // 384 + x) % 4 * 384 + cid % 384
    start = jnp.where(l == 0, grad, (rows == cols).astype(f32))

    y, yb = start, start.astype(bf16)
    for _ in range(7):
        stats, y, yb = step(stats, y, yb, start, f_own, f_oth)

    x, k, l, same, yb = lax.optimization_barrier((x, k, l, same, yb))
    yb = lax.dynamic_slice_in_dim(jnp.concatenate([yb, yb], 1), (4 - x) * 384, 1536, 1)
    zp = jnp.stack([yb[:, 384 * c : 384 * c + 384] for c in range(4)])
    zp = lax.all_to_all(zp, "x", split_axis=0, concat_axis=0, tiled=True)
    zp = [permute(zp, ("l", "k", "h"), lambda c, t=t: {"l": t, "k": c["h"], "h": c["k"]} if c["l"] == 0 else None) for t in (0, 1)]
    zp = jnp.where(l == 0, zp[0], zp[1])
    zall = lax.all_gather(zp, "z", axis=1, tiled=True)
    def p1(c):
        return None if c["l"] == 0 else {"l": c["h"], "h": c["h"]}
    def p2(c):
        return None if c["l"] == 0 else {"l": c["h"], "h": 1 - c["h"]}
    w1 = permute(yb, ("l", "h"), p1)
    w2 = permute(yb, ("l", "h"), p2)
    wp = jnp.where(l == h, w1, w2)
    wx = copies_over(wp, "x")
    acc = dot(wx.reshape(192, 1536), zall.reshape(1536, 384))
    acc = acc.reshape(2, 96, 384)
    keep = lax.dynamic_index_in_dim(acc, k, 0, keepdims=False)
    give = lax.dynamic_index_in_dim(acc, 1 - k, 0, keepdims=False)
    pre = keep + shift(give, "k", 1)
    total = jnp.full((8, 128), jnp.sum(pre * pre))
    for rest in (("z", "l"), ("k", "h", "x")):
        total = jnp.sum(copies_over(total, rest), 0)
    return pre * lax.rsqrt(total[:1, :1] / (D * D) + epsilon)


def solution(mesh):
    split = Mesh(mesh.devices.reshape(8, 2, 2, 2, 4), AXES)
    return jax.shard_map(
        shards,
        mesh=split,
        in_specs=(P(("z", "l", "k"), ("h", "x")),) * 2,
        out_specs=P(("z", "l", "k"), ("h", "x")),
        check_vma=False,
    )
```

```python
import functools
import itertools
import jax
import jax.numpy as jnp
from jax import lax
from jax.experimental import pallas as pl
from jax.experimental.pallas import tpu as pltpu
from jax.sharding import Mesh
from jax.sharding import PartitionSpec as P

D = 3072
NA = 16
VLIM = 50
AXES = ("z", "l", "k", "h", "x")
damping = 0.05
epsilon = 1e-06
bf16 = jnp.bfloat16
f32 = jnp.float32


def permute(t, axes, move):
    axes = tuple(a for a in AXES if a in axes)
    sizes = [lax.axis_size(a) for a in axes]

    def flat(c):
        r = 0
        for ci, s in zip(c, sizes):
            r = r * s + ci
        return r

    pairs = []
    for c in itertools.product(*[range(s) for s in sizes]):
        d = move(dict(zip(axes, c)))
        if d is not None:
            pairs.append((flat(c), flat([d[a] for a in axes])))
    return lax.ppermute(t, axes if len(axes) > 1 else axes[0], pairs)


def shift(t, axis, by):
    n = lax.axis_size(axis)
    if by % n == 0:
        return t
    return permute(t, (axis,), lambda c: {axis: (c[axis] + by) % n})


def tdot(a, b):
    return lax.dot_general(a, b, (((0,), (0,)), ((), ())), preferred_element_type=f32)


def dot(a, b):
    return jnp.dot(a, b, preferred_element_type=f32)


def absolute(pieces, index, n):
    out = jnp.zeros((n, *pieces[0].shape), pieces[0].dtype)
    for j, p in enumerate(pieces):
        out = lax.dynamic_update_index_in_dim(out, p, (index - j) & (n - 1), 0)
    return out


def copies_over(t, axes):
    copies = jnp.broadcast_to(t, (lax.axis_size(axes), *t.shape))
    return lax.all_to_all(copies, axes, split_axis=0, concat_axis=0, tiled=True)


def products_kernel(js, *refs):
    n = len(js)
    b_refs, (r_ref, r2_ref) = refs[: 2 * n], refs[2 * n : 2 * n + 2]
    out_ref, whole, sem = refs[-3:]
    copies = []
    for t, j in enumerate(js):
        b_ref, b2_ref = b_refs[2 * t : 2 * t + 2]

        @pl.loop(0, 3)
        def _(q):
            at = pl.ds(pl.multiple_of(384 * jnp.minimum(q, 1), 128), 384)
            p = dot(b_ref[at, :], r_ref[q & 1]) + dot(b2_ref[at, :], r2_ref[q & 1])
            whole[3 * t + q] = p.astype(bf16).reshape(8, 48, 384)

        for q in range(3):
            copies.append(pltpu.make_async_copy(whole.at[3 * t + q], out_ref.at[:, q, j], sem.at[3 * t + q]))
            copies[-1].start()
    for cp in copies:
        cp.wait()


def products(js, part, *operands):
    vmem = pl.BlockSpec(memory_space=pltpu.VMEM)
    hbm = pl.BlockSpec(memory_space=pltpu.HBM)
    more = () if part is None else (part,)
    n = len(js)
    return pl.pallas_call(
        functools.partial(products_kernel, js),
        out_shape=pltpu.HBM((8, 3, 4, 48, 384), bf16),
        in_specs=[vmem] * len(operands) + [hbm] * len(more),
        out_specs=hbm,
        scratch_shapes=[
            pltpu.VMEM((3 * n, 8, 48, 384), bf16),
            pltpu.SemaphoreType.DMA((3 * n,)),
        ],
        input_output_aliases={len(operands): 0} if more else {},
        compiler_params=pltpu.CompilerParams(vmem_limit_bytes=24 * 2**20),
        cost_estimate=pl.CostEstimate(flops=9 * 10**8 * n, bytes_accessed=4 * 10**6 * n, transcendentals=0),
    )(*operands, *more)


def assemble_kernel(*refs):
    x_ref, a_refs, b_ref = refs[0], refs[1:5], refs[5]
    own_ref, oth_ref, stats_ref, sem_in = refs[6:]
    whole = (own_ref, oth_ref)
    x = x_ref[0]
    loads = []
    for hf in range(2):
        for r in range(4):
            for c in range(4):
                j = (c - r) % 4
                at = 16 * hf + 4 * r + c
                slabs, cols = pl.ds(8 * r, 8), pl.ds(384 * c, 384)
                dst = whole[hf].at[slabs, pl.ds(0, NA), cols]
                loads.append(pltpu.make_async_copy(a_refs[c].at[hf, :, j], dst, sem_in.at[2 * at]))
                dst = whole[hf].at[slabs, pl.ds(NA, 48 - NA), cols]
                loads.append(pltpu.make_async_copy(b_ref.at[:, lax.rem(x + c, 4), hf, j], dst, sem_in.at[2 * at + 1]))
    for cp in loads:
        cp.start()
    row = lax.broadcasted_iota(jnp.int32, (16, 384), 0)
    col = lax.broadcasted_iota(jnp.int32, (16, 384), 1)
    stats_ref[...] = jnp.zeros_like(stats_ref)
    for hf in range(2):
        for r in range(4):
            base = 8 * r
            for i in range(8):
                loads[8 * (4 * hf + r) + i].wait()

            def add(i, acc):
                sq, tr = acc
                for t in range(3):
                    v = whole[hf][base + i, 16 * t : 16 * t + 16, :].astype(f32)
                    sq = sq + v * v
                    if hf == 0:
                        d = whole[hf][base + i, 16 * t : 16 * t + 16, 384 * r : 384 * r + 384].astype(f32)
                        tr = tr + jnp.where(col == row + (48 * i + 16 * t), d, 0.0)
                return sq, tr

            zero = (jnp.zeros((16, 1536), f32), jnp.zeros((16, 384), f32))
            sq, tr = lax.fori_loop(0, 8, add, zero)
            sq = sum(sq[:, 128 * i : 128 * i + 128] for i in range(12))
            tr = sum(tr[:, 128 * i : 128 * i + 128] for i in range(3))
            stats_ref[0:8, :] += tr[:8] + tr[8:]
            stats_ref[8:16, :] += sq[:8] + sq[8:]


def assemble(x, got_a, got_b):
    hbm = pl.BlockSpec(memory_space=pltpu.HBM)
    half = pltpu.VMEM((32, 48, 1536), bf16)
    own, oth, stats = pl.pallas_call(
        assemble_kernel,
        out_shape=(half, half, jax.ShapeDtypeStruct((16, 128), f32)),
        in_specs=[pl.BlockSpec(memory_space=pltpu.SMEM)] + [hbm] * 5,
        out_specs=[pl.BlockSpec(memory_space=pltpu.VMEM)] * 3,
        scratch_shapes=[
            pltpu.SemaphoreType.DMA((64,)),
        ],
        compiler_params=pltpu.CompilerParams(vmem_limit_bytes=VLIM * 2**20),
        cost_estimate=pl.CostEstimate(flops=10**7, bytes_accessed=19 * 10**6, transcendentals=0),
    )(x.reshape(1), *got_a, got_b)
    return own, oth, stats


def own_kernel(yb_ref, f_ref, out_ref):
    @pl.loop(0, 1536, step=768)
    def _(i):
        at = pl.ds(pl.multiple_of(i, 768), 768)
        out_ref[:, at] = dot(yb_ref[...], f_ref[:, :, at].reshape(1536, 768))


def rest_kernel(first, *refs):
    if first:
        st_ref, st2_ref, yb_ref, f_ref, part_ref, y_ref, start_ref, out_ref, outb_ref, coef_ref = refs
        st = st_ref[...] + st2_ref[...]
        trace = jnp.sum(st[:8], keepdims=True)
        square = jnp.sum(st[8:], keepdims=True)
        damp = damping * trace / D
        scale = lax.rsqrt(square + 2.0 * damp * trace + D * damp * damp)
        coef_ref[0:8, :] = jnp.broadcast_to(scale, (8, 128))
        coef_ref[8:16, :] = jnp.broadcast_to(damp, (8, 128))
    else:
        coef_ref, yb_ref, f_ref, part_ref, y_ref, start_ref, out_ref, outb_ref = refs
        scale, damp = coef_ref[0:1, 0:1], coef_ref[8:9, 0:1]

    @pl.loop(0, 1536, step=512)
    def _(i):
        at = pl.ds(pl.multiple_of(i, 512), 512)
        prod = dot(yb_ref[...], f_ref[:, :, at].reshape(1536, 512)) + part_ref[:, at]
        y = y_ref[:, at]
        y = start_ref[:, at] + y - scale * (prod + damp * y)
        out_ref[:, at] = y
        outb_ref[:, at] = y.astype(bf16)


def step(coef, y, yb, start, f_own, f_oth):
    first = len(coef) == 2
    vmem = pl.BlockSpec(memory_space=pltpu.VMEM)
    limit = pltpu.CompilerParams(vmem_limit_bytes=16 * 2**20)
    cost = pl.CostEstimate(flops=2 * 48 * 1536 * 1536, bytes_accessed=6 * 10**6, transcendentals=0)
    yo = shift(yb, "k", 1)
    part = pl.pallas_call(
        own_kernel,
        out_shape=jax.ShapeDtypeStruct((48, 1536), f32),
        in_specs=[vmem] * 2,
        out_specs=vmem,
        compiler_params=limit,
        cost_estimate=cost,
    )(yb, f_own)
    outs = [jax.ShapeDtypeStruct((48, 1536), f32), jax.ShapeDtypeStruct((48, 1536), bf16)]
    if first:
        outs.append(jax.ShapeDtypeStruct((16, 128), f32))
    y, yb, *made = pl.pallas_call(
        functools.partial(rest_kernel, first),
        out_shape=outs,
        in_specs=[vmem] * (5 + len(coef)),
        out_specs=[vmem] * len(outs),
        compiler_params=limit,
        cost_estimate=cost,
    )(*coef, yo, f_oth, part, y, start)
    return (made if first else coef), y, yb


def shards(act, cot):
    z, l, k, h, x = (lax.axis_index(a) for a in AXES)
    same = k == h
    flat = jnp.stack([act, cot])
    own = jnp.concatenate([act.T, cot.T], 0)
    up, down = shift(own, "x", 1), shift(own, "x", 3)
    other = shift(flat, "h", 1)
    far = shift(up[:384], "x", 1), shift(down[384:], "x", 3)
    own2, up2, flat2, other2 = (shift(b, "k", 1) for b in (own, up, flat, other))
    right = jnp.where(same, flat, other)
    right2 = jnp.where(same, flat2, other2)
    part = products((0, 1, 3), None, own, own2, up, up2, down, shift(down, "k", 1), right, right2)
    far, part = lax.optimization_barrier((far, part))
    far = jnp.concatenate(far, 0)
    part = products((2,), part, far, shift(far, "k", 1), right, right2)
    tile = lax.psum_scatter(part, "z", scatter_dimension=0, tiled=False)
    fa, fg, fw = tile[0], tile[1], tile[2]
    mine, give = jnp.where(l == 0, fa, fg), jnp.where(l == 0, fg, fa)
    diagonal = lambda c: {"l": 1 - c["l"], "h": 1 - c["h"]}
    sent = shift(give, "l", 1)
    near = shift(mine[:, NA:], "h", 1)
    sent_near = permute(give[:, NA:], ("l", "h"), diagonal)
    sent, near, sent_near = lax.optimization_barrier((sent, near, sent_near))
    mine = (mine.astype(f32) + sent.astype(f32)).astype(bf16)
    v = (near.astype(f32) + sent_near.astype(f32)).astype(bf16)

    ta, tb = mine[:, :NA], mine[:, NA:]
    g = jnp.stack([jnp.where(same, tb, v), jnp.where(same, v, tb)])
    g = copies_over(g, "x")
    fw, g = lax.optimization_barrier((fw, g))
    got_b = lax.all_gather(g, "z", axis=0, tiled=False)
    u = lax.all_gather(ta, "z", axis=0, tiled=False)
    v = shift(u, "h", 1)
    u = jnp.stack([jnp.where(same, u, v), jnp.where(same, v, u)])
    left, right = shift(u, "x", 1), shift(u, "x", 3)
    across = jnp.concatenate([shift(left[:1], "x", 1), shift(right[1:], "x", 3)], 0)
    got_a = [u, right, across, left]
    fw = fw.astype(f32) + shift(fw, "l", 1).astype(f32)
    f_own, f_oth, stats = assemble(x, got_a, got_b)
    stats = (stats, shift(stats, "k", 1))

    grad = absolute([fw[j] for j in range(4)], x, 4)
    grad = lax.all_to_all(grad, "x", split_axis=0, concat_axis=0, tiled=True)
    grad = jnp.concatenate([grad[c % 4] for c in range(8)], 1)
    grad = lax.dynamic_slice_in_dim(grad, x * 384, 1536, 1)
    rows = 384 * z + 192 * h + 48 * x + lax.broadcasted_iota(jnp.int32, (48, 1536), 0)
    cid = lax.broadcasted_iota(jnp.int32, (48, 1536), 1)
    cols = 1536 * k + (cid // 384 + x) % 4 * 384 + cid % 384
    start = jnp.where(l == 0, grad, (rows == cols).astype(f32))

    y, yb = start, start.astype(bf16)
    for _ in range(7):
        stats, y, yb = step(stats, y, yb, start, f_own, f_oth)

    x, k, l, same, yb = lax.optimization_barrier((x, k, l, same, yb))
    yb = lax.dynamic_slice_in_dim(jnp.concatenate([yb, yb], 1), (4 - x) * 384, 1536, 1)
    zp = jnp.stack([yb[:, 384 * c : 384 * c + 384] for c in range(4)])
    zp = lax.all_to_all(zp, "x", split_axis=0, concat_axis=0, tiled=True)
    zp = [permute(zp, ("l", "k", "h"), lambda c, t=t: {"l": t, "k": c["h"], "h": c["k"]} if c["l"] == 0 else None) for t in (0, 1)]
    zp = jnp.where(l == 0, zp[0], zp[1])
    zall = lax.all_gather(zp, "z", axis=1, tiled=True)
    def p1(c):
        return None if c["l"] == 0 else {"l": c["h"], "h": c["h"]}
    def p2(c):
        return None if c["l"] == 0 else {"l": c["h"], "h": 1 - c["h"]}
    w1 = permute(yb, ("l", "h"), p1)
    w2 = permute(yb, ("l", "h"), p2)
    wp = jnp.where(l == h, w1, w2)
    wx = copies_over(wp, "x")
    acc = dot(wx.reshape(192, 1536), zall.reshape(1536, 384))
    acc = acc.reshape(2, 96, 384)
    keep = lax.dynamic_index_in_dim(acc, k, 0, keepdims=False)
    give = lax.dynamic_index_in_dim(acc, 1 - k, 0, keepdims=False)
    pre = keep + shift(give, "k", 1)
    total = jnp.full((8, 128), jnp.sum(pre * pre))
    for rest in (("z", "k"), ("l", "h", "x")):
        total = jnp.sum(copies_over(total, rest), 0)
    return pre * lax.rsqrt(total[:1, :1] / (D * D) + epsilon)


def solution(mesh):
    split = Mesh(mesh.devices.reshape(8, 2, 2, 2, 4), AXES)
    return jax.shard_map(
        shards,
        mesh=split,
        in_specs=(P(("z", "l", "k"), ("h", "x")),) * 2,
        out_specs=P(("z", "l", "k"), ("h", "x")),
        check_vma=False,
    )
```
